128 devices in a mesh: tm: 8 (over y, z_lo), dp: 16 (over x, z_hi, core).
Axes of the slice: x: 4, y: 4, z: 4 (z_hi: 2, z_lo: 2; z = z_hi * 2 + z_lo), core: 2. Of those that a mesh axis runs over, the one named last changes fastest.
Arguments:
- features: bfloat16 [16, 16, 16, 24, 384], P('dp', 'tm'), may hold values from -60 to 60
- conv_weight: bfloat16 [10368, 384], replicated, may hold values from -0.0625 to 0.0625
- up_weight: bfloat16 [1152, 768], replicated, may hold values from -0.1875 to 0.1875
- cotangent: bfloat16 [16, 32, 16, 24, 384], P('dp', 'tm'), may hold values from -6 to 6
Outputs:
- features_grad: bfloat16 [16, 16, 16, 24, 384], P('dp', 'tm')
- grad_conv: float32 [10368, 384], P('dp', 'tm')
- grad_up: float32 [1152, 768], P('dp', 'tm')
The draws below stay inside these ranges and needn't reach their ends.
All inputs are finite; a program needn't handle non-finite values.
Results may differ from the reference program's by a relative error of at most 0.0049.
Values may be sent and summed in bfloat16 or wider, within the bound.
No kernel may reach another device: no remote copies, remote signals or barrier semaphores. Data moves between devices by JAX's collectives and lax.ppermute only.
A program may use at most 128 MiB of HBM per device.

```python
import math
import jax
import jax.numpy as jnp
from jax import lax

C = 384
G = 32
HT = 16
WD = 24
CROPS = 16
LFRAMES = 16
POSITIONS = 98304


def draw_features(key, part):
    first, second, third = jax.random.split(key, 3)
    shape = (CROPS, LFRAMES, HT, WD, C)
    base = jnp.clip(jax.random.normal(first, shape, jnp.float32), -6.0, 6.0)
    pixel = jnp.exp(jax.random.uniform(second, (CROPS, LFRAMES, HT, WD, 1), jnp.float32, 0.0, 2.3))
    channel = jnp.exp(jax.random.uniform(third, (C,), jnp.float32, 0.0, 2.3))
    return (base * pixel * channel * 0.1).astype(jnp.bfloat16)


def level_of(own_key, extent, pieces, smallest, largest):
    gain, own = 1.0, jax.random.fold_in(own_key, 6)
    for axis_at, blocks in pieces:
        heights = jnp.exp(jax.random.uniform(jax.random.fold_in(own, axis_at), (blocks,), jnp.float32, smallest / len(pieces), largest / len(pieces)))
        gain = gain * jnp.repeat(heights, extent[axis_at] // blocks).reshape([-1 if axis == axis_at else 1 for axis in range(len(extent))])
    return gain


def centred(key, shape, scale, limit, pieces=(), kind=jnp.bfloat16):
    values = scale * jax.random.normal(key, shape, jnp.float32)
    if pieces:
        values = values * level_of(key, shape, pieces, -0.22, 0.18)
    return jnp.clip(values, -limit, limit).astype(kind)


def setup_inputs(seed: int = 0) -> dict:
    key_list = jax.random.split(jax.random.key(seed), 5)
    return {
        "features": draw_features(jax.random.fold_in(key_list[4], 71), 0),
        "conv_weight": centred(key_list[1], (27 * C, C), (27 * C) ** -0.5, 0.0625),
        "up_weight": centred(key_list[2], (3 * C, 2 * C), (3 * C) ** -0.5, 0.1875),
        "cotangent": centred(key_list[3], (CROPS, 2 * LFRAMES, HT, WD, C), 1.0, 6.0, ((0, 16), (1, 8))),
    }


EPSILON = 1e-06

def norm_act(field):
    shape = field.shape
    grouped = field.reshape(shape[:-3] + (shape[-3] * shape[-2], G, shape[-1] // G))
    center = grouped - lax.optimization_barrier(jnp.mean(grouped, axis=(-3, -1), keepdims=True))
    spread = lax.optimization_barrier(jnp.mean(center * center, axis=(-3, -1), keepdims=True))
    normed = center * lax.rsqrt(spread + EPSILON)
    return jax.nn.silu(normed).reshape(shape)

def reference(features, conv_weight, up_weight, cotangent):
    kernel = conv_weight.reshape(3, 3, 3, C, C)
    up_kernel = up_weight.reshape(3, C, 2 * C)

    def per_crop(totals, inputs):
        clip, clip_grad = inputs
        field = clip.astype(jnp.float32)
        act_float, pullback = jax.vjp(norm_act, field)
        act = act_float.astype(jnp.bfloat16)
        act_pad = jnp.pad(act, ((2, 0), (1, 1), (1, 1), (0, 0)))
        conv_out = jnp.zeros((LFRAMES * HT * WD, C), jnp.float32)
        for time_tap in range(3):
            for high_tap in range(3):
                for wide_tap in range(3):
                    window = act_pad[time_tap:time_tap + LFRAMES, high_tap:high_tap + HT, wide_tap:wide_tap + WD].reshape(-1, C)
                    conv_out = conv_out + jnp.dot(window, kernel[time_tap, high_tap, wide_tap], preferred_element_type=jnp.float32)
        hidden = (field.reshape(-1, C) + conv_out).astype(jnp.bfloat16).reshape(LFRAMES, HT, WD, C)
        up_grad = clip_grad.reshape(LFRAMES, 2, HT, WD, C).transpose(0, 2, 3, 1, 4).reshape(LFRAMES, HT, WD, 2 * C)
        hidden_pad = jnp.pad(hidden, ((2, 0), (0, 0), (0, 0), (0, 0)))
        up_pad = jnp.pad(up_grad, ((0, 2), (0, 0), (0, 0), (0, 0)))
        up_flat = up_grad.reshape(-1, 2 * C)
        hidden_grad = jnp.zeros((LFRAMES * HT * WD, C), jnp.float32)
        up_terms = []
        for tap in range(3):
            hidden_grad = hidden_grad + jnp.dot(up_pad[tap:tap + LFRAMES].reshape(-1, 2 * C), up_kernel[2 - tap].T, preferred_element_type=jnp.float32)
            up_terms.append(jnp.dot(hidden_pad[tap:tap + LFRAMES].reshape(-1, C).T, up_flat, preferred_element_type=jnp.float32))
        conv_grad = hidden_grad.astype(jnp.bfloat16)
        grad_pad = jnp.pad(conv_grad.reshape(LFRAMES, HT, WD, C), ((0, 2), (1, 1), (1, 1), (0, 0)))
        act_grad = jnp.zeros((LFRAMES * HT * WD, C), jnp.float32)
        conv_terms = []
        for time_tap in range(3):
            for high_tap in range(3):
                for wide_tap in range(3):
                    later = grad_pad[2 - time_tap:2 - time_tap + LFRAMES, 2 - high_tap:2 - high_tap + HT, 2 - wide_tap:2 - wide_tap + WD].reshape(-1, C)
                    act_grad = act_grad + jnp.dot(later, kernel[time_tap, high_tap, wide_tap].T, preferred_element_type=jnp.float32)
                    window = act_pad[time_tap:time_tap + LFRAMES, high_tap:high_tap + HT, wide_tap:wide_tap + WD].reshape(-1, C)
                    conv_terms.append(jnp.dot(window.T, conv_grad, preferred_element_type=jnp.float32))
        norm_grad, = pullback(act_grad.reshape(LFRAMES, HT, WD, C))
        clip_out = (hidden_grad.reshape(LFRAMES, HT, WD, C) + norm_grad).astype(jnp.bfloat16)
        return ((totals[0] + jnp.concatenate(conv_terms, axis=0), totals[1] + jnp.concatenate(up_terms, axis=0)), clip_out)
    initial = (jnp.zeros((27 * C, C), jnp.float32), jnp.zeros((3 * C, 2 * C), jnp.float32))
    (conv_total, up_total), features_grad = lax.scan(per_crop, initial, (features, cotangent))
    scale = 1.0 / math.sqrt(POSITIONS)
    return (features_grad, conv_total * scale, up_total * scale)
```

```python
import math

import jax
import jax.numpy as jnp
from jax import lax
from jax.sharding import PartitionSpec as P

G = 32


EPSILON = 1e-06


def from_behind(value, axis, steps):
    count = lax.axis_size(axis)
    first, last = (max(0, -steps), min(count, count - steps))
    return lax.ppermute(value, axis, [(source, source + steps) for source in range(first, last)])


def norm_act(field):
    shape = field.shape
    grouped = field.reshape(shape[:-3] + (shape[-3] * shape[-2], G, shape[-1] // G))
    center = grouped - jnp.mean(grouped, axis=(-3, -1), keepdims=True)
    spread = jnp.mean(center * center, axis=(-3, -1), keepdims=True)
    normed = center * lax.rsqrt(spread + EPSILON)
    return jax.nn.silu(normed).reshape(shape)


def space_pad(field):
    return jnp.pad(field, ((0, 0), (0, 0), (1, 1), (1, 1), (0, 0)))


def stack_taps(padded, frames, height, breadth):
    pieces = [
        padded[
            :,
            time_tap : time_tap + frames,
            high_tap : high_tap + height,
            wide_tap : wide_tap + breadth,
            :,
        ]
        for time_tap in range(3)
        for high_tap in range(3)
        for wide_tap in range(3)
    ]
    joined = jnp.concatenate(pieces, axis=-1)
    return joined.reshape(-1, joined.shape[-1])


def stack_times(padded, frames):
    pieces = [padded[:, time_tap : time_tap + frames] for time_tap in range(3)]
    joined = jnp.concatenate(pieces, axis=-1)
    return joined.reshape(-1, joined.shape[-1])


def contract_rows(left, right):
    return lax.dot_general(
        left, right, (((0,), (0,)), ((), ())), preferred_element_type=jnp.float32
    )


def reduce_blocks(partial):
    rows, cols = partial.shape
    data, times = lax.axis_size("dp"), lax.axis_size("tm")
    chips = data // 2
    core = lax.axis_index("dp") % 2
    halves = partial.reshape(chips, 2, rows // data, cols)
    send = lax.dynamic_index_in_dim(halves, 1 - core, 1, keepdims=False).astype(jnp.bfloat16)
    keep = lax.dynamic_index_in_dim(halves, core, 1, keepdims=False)
    swapped = lax.ppermute(send, "dp", [(d, d ^ 1) for d in range(data)])
    pair = (keep + swapped.astype(jnp.float32)).astype(jnp.bfloat16)
    groups = [[2 * chip + side for chip in range(chips)] for side in range(2)]
    spread = lax.all_to_all(pair, "dp", 0, 0, axis_index_groups=groups, tiled=True)
    rowsum = jnp.sum(spread.astype(jnp.float32), axis=0).astype(jnp.bfloat16)
    blocks = rowsum.reshape(rows // data, times, cols // times).transpose(1, 0, 2)
    final = lax.all_to_all(blocks, "tm", 0, 0, tiled=True)
    return jnp.sum(final.astype(jnp.float32), axis=0)


def shards(features, conv_weight, up_weight, cotangent):
    crop_count, frames, height, breadth, channels = features.shape
    block_shape = features.shape
    feature_field = features.astype(jnp.float32)
    act_float, pullback = jax.vjp(norm_act, feature_field)
    act = act_float.astype(jnp.bfloat16)
    act_prior = from_behind(act, "tm", 1)
    act_cols = stack_taps(
        space_pad(jnp.concatenate([act_prior, act], axis=1)), frames, height, breadth
    )
    conv_out = jnp.dot(act_cols, conv_weight, preferred_element_type=jnp.float32)
    hidden = (
        (feature_field.reshape(-1, channels) + conv_out).astype(jnp.bfloat16).reshape(block_shape)
    )
    up_grad = cotangent.reshape(crop_count, frames, 2, height, breadth, channels)
    up_grad = up_grad.transpose(0, 1, 3, 4, 2, 5).reshape(
        crop_count, frames, height, breadth, 2 * channels
    )
    up_next = from_behind(up_grad, "tm", -1)
    up_cols = stack_times(jnp.concatenate([up_grad, up_next], axis=1), frames)
    up_flip = (
        up_weight.reshape(3, channels, 2 * channels)[::-1]
        .transpose(0, 2, 1)
        .reshape(6 * channels, channels)
    )
    hidden_grad = jnp.dot(up_cols, up_flip, preferred_element_type=jnp.float32)
    conv_grad = hidden_grad.astype(jnp.bfloat16)
    conv_field = conv_grad.reshape(block_shape)
    conv_next = from_behind(conv_field, "tm", -1)
    conv_cols = stack_taps(
        space_pad(jnp.concatenate([conv_field, conv_next], axis=1)), frames, height, breadth
    )
    conv_flip = (
        conv_weight.reshape(3, 3, 3, channels, channels)[::-1, ::-1, ::-1]
        .transpose(0, 1, 2, 4, 3)
        .reshape(27 * channels, channels)
    )
    act_grad = jnp.dot(conv_cols, conv_flip, preferred_element_type=jnp.float32)
    (norm_grad,) = pullback(act_grad.reshape(block_shape))
    features_grad = (hidden_grad.reshape(block_shape) + norm_grad).astype(jnp.bfloat16)
    data_count = lax.axis_size("dp")
    time_count = lax.axis_size("tm")
    scale = 1.0 / math.sqrt(crop_count * frames * height * breadth * data_count * time_count)
    grad_conv = reduce_blocks(contract_rows(act_cols, conv_grad)) * scale
    hidden_flat = hidden.reshape(-1, channels)
    up_ext = jnp.concatenate([up_grad, up_next], axis=1)
    up_part = jnp.concatenate(
        [
            contract_rows(hidden_flat, up_ext[:, 2 - k : 2 - k + frames].reshape(-1, 2 * channels))
            for k in range(3)
        ],
        axis=0,
    )
    grad_up = reduce_blocks(up_part) * scale
    return (features_grad, grad_conv, grad_up)


def solution(mesh):
    in_specs = (P("dp", "tm", None, None, None), P(), P(), P("dp", "tm", None, None, None))
    out_specs = (P("dp", "tm", None, None, None), P("dp", "tm"), P("dp", "tm"))
    return jax.shard_map(shards, mesh=mesh, in_specs=in_specs, out_specs=out_specs, check_vma=False)
```

```python
import math

import jax
import jax.numpy as jnp
from jax import lax
from jax.experimental import pallas as pl
from jax.experimental.pallas import tpu as pltpu
from jax.sharding import PartitionSpec as P


G = 32
EPSILON = 1e-06
F32 = jnp.float32
BF16 = jnp.bfloat16
ROW_ROW = (((1,), (1,)), ((), ()))


def call(body, grid, ins, outs, shapes, scratch=(), flops=0, nbytes=0):
    return pl.pallas_call(
        body,
        grid=grid,
        in_specs=ins,
        out_specs=outs,
        out_shape=shapes,
        scratch_shapes=list(scratch),
        cost_estimate=pl.CostEstimate(flops=flops, bytes_accessed=nbytes, transcendentals=0),
        compiler_params=pltpu.CompilerParams(
            dimension_semantics=("arbitrary",) * len(grid), vmem_limit_bytes=56 * 2**20
        ),
    )


def whole(*shape):
    return pl.BlockSpec(shape, lambda *at: (0,) * len(shape))


def from_behind(value, axis, steps):
    count = lax.axis_size(axis)
    first, last = (max(0, -steps), min(count, count - steps))
    return lax.ppermute(value, axis, [(source, source + steps) for source in range(first, last)])


def group_mean(value):
    rows, channels = value.shape
    width = channels // G
    sums = jnp.broadcast_to(jnp.sum(value, axis=0, keepdims=True), (8, channels))
    left = lax.broadcasted_iota(jnp.int32, (channels, channels), 0) // width
    right = lax.broadcasted_iota(jnp.int32, (channels, channels), 1) // width
    mix = jnp.where(left == right, 1.0, 0.0).astype(F32)
    total = jnp.dot(sums, mix, precision=lax.Precision.HIGHEST, preferred_element_type=F32)
    return total[0:1] * (1.0 / (rows * width))


def normalize(value):
    center = value - group_mean(value)
    scale = lax.rsqrt(group_mean(center * center) + EPSILON)
    return center * scale, scale


def act_body(field_ref, act_ref):
    normed, _ = normalize(field_ref[0].astype(F32))
    act_ref[0] = (normed / (1.0 + jnp.exp(-normed))).astype(BF16)


def up_body(cot_ref, weight_ref, local_ref, prior_ref):
    channels = cot_ref.shape[-1]
    weight = weight_ref[...]
    parts = []
    for frame in range(2):
        pair = jnp.concatenate([cot_ref[2 * frame], cot_ref[2 * frame + 1]], axis=1)
        parts.append(lax.dot_general(pair, weight, ROW_ROW, preferred_element_type=F32))
    first, second = parts
    low, mid, high = (slice(k * channels, (k + 1) * channels) for k in range(3))
    local_ref[0] = first[:, high] + second[:, mid]
    local_ref[1] = second[:, high]
    prior_ref[0] = first[:, low].astype(BF16)
    prior_ref[1] = (first[:, mid] + second[:, low]).astype(BF16)


def turn_body(weight_ref, out_ref):
    for tap in range(3):
        out_ref[tap] = weight_ref[2 - tap].astype(F32).T.astype(BF16)


def fill_shifts(frames, cols_ref, breadth):
    rows, channels = frames[0].shape
    place = lax.broadcasted_iota(jnp.int32, (rows, channels), 0)
    wide = place % breadth
    for at, frame in enumerate(frames):
        value = frame.astype(F32)
        for wide_tap in range(3):
            moved = value
            if wide_tap != 1:
                moved = pltpu.roll(value, (1 - wide_tap) % rows, 0)
                edge = 0 if wide_tap == 0 else breadth - 1
                moved = jnp.where(wide == edge, 0.0, moved)
            for high_tap in range(3):
                shifted = moved
                if high_tap == 0:
                    shifted = jnp.concatenate(
                        [jnp.zeros((breadth, channels), F32), moved[: rows - breadth]], axis=0
                    )
                elif high_tap == 2:
                    shifted = jnp.concatenate(
                        [moved[breadth:], jnp.zeros((breadth, channels), F32)], axis=0
                    )
                tap = high_tap * 3 + wide_tap
                cols_ref[at * rows : (at + 1) * rows, tap * channels : (tap + 1) * channels] = (
                    shifted.astype(BF16)
                )


def accumulate(step, weight_ref, cols_ref, acc_ref):
    rows = acc_ref.shape[0]
    part = jnp.dot(
        cols_ref[pl.ds(pl.multiple_of(step * (rows // 2), rows // 2), rows), :],
        weight_ref[0],
        preferred_element_type=F32,
    )

    @pl.when(step == 0)
    def _():
        acc_ref[...] = part

    @pl.when(step > 0)
    def _():
        acc_ref[...] += part


def make_conv(breadth):
    def body(early_ref, late_ref, weight_ref, field_ref, hidden_ref, cols_ref, acc_ref):
        step = pl.program_id(0)

        @pl.when(step == 0)
        def _():
            frames = [early_ref[0], early_ref[1], late_ref[0], late_ref[1]]
            fill_shifts(frames, cols_ref, breadth)

        accumulate(step, weight_ref, cols_ref, acc_ref)

        @pl.when(step == 2)
        def _():
            rows = acc_ref.shape[0] // 2
            for frame in range(2):
                total = field_ref[frame].astype(F32) + acc_ref[frame * rows : (frame + 1) * rows]
                hidden_ref[frame] = total.astype(BF16)

    return body


def make_back(breadth):
    def body(
        early_ref, late_ref, weight_ref, field_ref, local_ref, next_ref, out_ref, cols_ref, acc_ref
    ):
        step = pl.program_id(0)

        @pl.when(step == 0)
        def _():
            frames = [early_ref[0], early_ref[1], late_ref[0], late_ref[1]]
            fill_shifts(frames, cols_ref, breadth)

        accumulate(step, weight_ref, cols_ref, acc_ref)

        @pl.when(step == 2)
        def _():
            rows = acc_ref.shape[0] // 2
            for frame in range(2):
                normed, scale = normalize(field_ref[frame].astype(F32))
                gate = 1.0 / (1.0 + jnp.exp(-normed))
                slope = gate * (1.0 + normed * (1.0 - gate))
                grad = acc_ref[frame * rows : (frame + 1) * rows] * slope
                inner = grad - group_mean(grad) - normed * group_mean(grad * normed)
                hidden_grad = local_ref[frame] + next_ref[frame].astype(F32)
                out_ref[frame] = (hidden_grad + scale * inner).astype(BF16)

    return body


def split_store(part, side, send_ref, keep_ref, times, at):
    rows, width = part.shape
    halves = part.reshape(times, rows // times, width)
    low = halves[:, : rows // times // 2]
    high = halves[:, rows // times // 2 :]
    send_ref[:, :, at : at + width] = jnp.where(side == 0, high, low).astype(BF16)
    keep_ref[:, :, at : at + width] = jnp.where(side == 0, low, high).astype(BF16)


def make_weight_grad(breadth, times):
    def body(side_ref, early_ref, late_ref, grad_ref, send_ref, keep_ref, cols_ref, turned_ref):
        step = pl.program_id(0)
        rows, channels = early_ref.shape[1:]

        @pl.when(step == 0)
        def _():
            frames = [early_ref[0], early_ref[1], late_ref[0], late_ref[1]]
            fill_shifts(frames, cols_ref, breadth)
            for frame in range(2):
                turned_ref[:, frame * rows : (frame + 1) * rows] = (
                    grad_ref[frame].astype(F32).T.astype(BF16)
                )

        start = pl.multiple_of(step * rows, rows)
        turned = turned_ref[...]
        total = cols_ref.shape[1]
        for at in range(0, total, 2 * channels):
            width = min(2 * channels, total - at)
            part = jnp.dot(
                turned,
                cols_ref[pl.ds(start, 2 * rows), at : at + width],
                preferred_element_type=F32,
            )
            split_store(part, side_ref[0], send_ref, keep_ref, times, at)

    return body


def make_up_grad(times):
    def body(side_ref, early_ref, late_ref, cot_ref, send_ref, keep_ref, cols_ref, turned_ref):
        rows, channels = early_ref.shape[1:]
        frames = [early_ref[0], early_ref[1], late_ref[0], late_ref[1]]
        for tap in range(3):
            for frame in range(2):
                cols_ref[
                    frame * rows : (frame + 1) * rows, tap * channels : (tap + 1) * channels
                ] = frames[frame + tap]
        for frame in range(2):
            for half in range(2):
                turned_ref[
                    half * channels : (half + 1) * channels, frame * rows : (frame + 1) * rows
                ] = cot_ref[2 * frame + half].astype(F32).T.astype(BF16)
        part = jnp.dot(turned_ref[...], cols_ref[...], preferred_element_type=F32)
        split_store(part, side_ref[0], send_ref, keep_ref, times, 0)

    return body


def swap_sides(value):
    return lax.ppermute(value, "dp", [(d, d ^ 1) for d in range(lax.axis_size("dp"))])


def place_of(device):
    time, data = divmod(device, 16)
    return [data // 4, time // 2, (data // 2 % 2) * 2 + time % 2, data % 2]


def device_at(x, y, z, core):
    return (y * 2 + z % 2) * 16 + x * 4 + z // 2 * 2 + core


def exchange(pieces, ring):
    got = [pieces[0]]
    for step in (1, 2, 3):
        pairs = []
        for device in range(128):
            place = place_of(device)
            place[ring] = (place[ring] + step) % 4
            pairs.append((device, device_at(*place)))
        got.append(lax.ppermute(pieces[step], ("tm", "dp"), pairs))
    return got


def added(refs):
    total = refs[0][...].astype(F32)
    for ref in refs[1:]:
        total = total + ref[...].astype(F32)
    return total


def join_body(place_ref, got_ref, keep_ref, *refs):
    row_refs, col_refs, hold_ref = refs[:4], refs[4:8], refs[8]
    step = pl.program_id(0)
    quarter = got_ref.shape[-1] // 4
    total = (got_ref[0].astype(F32) + keep_ref[0].astype(F32)).astype(BF16)
    for at in range(4):
        hold_ref[at] = total[0][:, at * quarter : (at + 1) * quarter]
    for slot in range(4):
        row_refs[slot][0] = hold_ref[lax.rem(place_ref[0] + slot, 4)]

        @pl.when(lax.rem(step - place_ref[1] + 4, 4) == slot)
        def _():
            col_refs[slot][...] = total[1]


def mid_body(place_ref, *refs):
    row_in, col_in, row_out, col_out = refs[:4], refs[4:8], refs[8:12], refs[12:16]
    row_hold, col_hold = refs[16:]
    quarter = col_in[0].shape[-1] // 4
    row_hold[...] = added(row_in).astype(BF16)
    total = added(col_in).astype(BF16)
    for at in range(4):
        col_hold[at] = total[:, at * quarter : (at + 1) * quarter]
    for slot in range(4):
        row_out[slot][...] = row_hold[lax.rem(place_ref[1] + slot, 4)]
        col_out[slot][...] = col_hold[lax.rem(place_ref[0] + slot, 4)]


def end_body(place_ref, *refs):
    outs, hold_ref = refs[8:12], refs[12]
    width = outs[0].shape[-1]
    for low in range(2):
        total = added(refs[4 * low : 4 * low + 4]).astype(BF16)
        for high in range(2):
            hold_ref[high * 2 + low] = total[:, high * width : (high + 1) * width]
    for slot in range(4):
        outs[slot][...] = hold_ref[lax.rem(place_ref[2] + slot, 4)]


def last_body(place_ref, *refs):
    total = added(refs[:4])
    width = total.shape[1] // 2
    low, high = total[:, :width], total[:, width:]
    refs[4][...] = jnp.where(place_ref[3] == 0, low, high)
    refs[5][...] = jnp.where(place_ref[3] == 0, high, low)


def reduce_blocks(send, keep):
    times, cols, rows = send.shape
    data, time = lax.axis_index("dp"), lax.axis_index("tm")
    place = jnp.stack([data // 4, time // 2, (data // 2 % 2) * 2 + time % 2, data % 2])
    place = place.astype(jnp.int32)
    scalars = pl.BlockSpec(memory_space=pltpu.SMEM)

    def small(body, arrays, shapes, scratch):
        return call(
            body,
            (1,),
            [scalars] + [whole(*array.shape) for array in arrays],
            [whole(*shape.shape) for shape in shapes],
            shapes,
            scratch,
            flops=1000,
            nbytes=2 * times * cols * rows,
        )(place, *arrays)

    def shape(*dims):
        return jax.ShapeDtypeStruct(dims, BF16)

    got = swap_sides(send)
    blocks = (4, 2, cols, rows)
    pair_spec = pl.BlockSpec((1, 2, cols, rows), lambda k: (k, 0, 0, 0))
    row_spec = pl.BlockSpec((1, cols, rows // 4), lambda k: (k, 0, 0))
    out = call(
        join_body,
        (4,),
        [scalars, pair_spec, pair_spec],
        [row_spec] * 4 + [whole(cols, rows)] * 4,
        [shape(4, cols, rows // 4)] * 4 + [shape(cols, rows)] * 4,
        [pltpu.VMEM((4, cols, rows // 4), BF16)],
        flops=1000,
        nbytes=6 * times * cols * rows,
    )(place, got.reshape(blocks), keep.reshape(blocks))
    first = exchange(out[4:], 1)
    second = exchange(out[:4], 0)
    hold = pltpu.VMEM((4, cols, rows // 4), BF16)
    out = small(mid_body, second + first, [shape(cols, rows // 4)] * 8, [hold, hold])
    first = exchange(out[:4], 1)
    second = exchange(out[4:], 0)
    hold = pltpu.VMEM((4, cols, rows // 8), BF16)
    out = small(end_body, first + second, [shape(cols, rows // 8)] * 4, [hold])
    out = exchange(out, 2)
    half = jax.ShapeDtypeStruct((cols, rows // 16), F32)
    mine, other = small(last_body, out, [half, half], [])
    got = swap_sides(other)
    side = data % 2
    full = jnp.where(
        side == 0, jnp.concatenate([mine, got], axis=0), jnp.concatenate([got, mine], axis=0)
    )
    return full.T


def join_pair(send, keep):
    swapped = swap_sides(send)
    return (keep.astype(F32) + swapped.astype(F32)).astype(BF16)


def over_times(pair):
    spread = lax.all_to_all(pair, "tm", 0, 0, tiled=True)
    return jnp.sum(spread.astype(F32), axis=0).astype(BF16)


def over_data(rowsum):
    cols, rows = rowsum.shape
    chips = lax.axis_size("dp") // 2
    side = lax.axis_index("dp") % 2
    blocks = rowsum.reshape(cols, chips, rows // chips).transpose(1, 0, 2)
    groups = [[2 * chip + own for chip in range(chips)] for own in range(2)]
    spread = lax.all_to_all(blocks, "dp", 0, 0, axis_index_groups=groups, tiled=True)
    total = jnp.sum(spread.astype(F32), axis=0).reshape(cols, 2, rows // chips // 2)
    mine = lax.dynamic_index_in_dim(total, side, 1, keepdims=False)
    other = lax.dynamic_index_in_dim(total, 1 - side, 1, keepdims=False)
    got = swap_sides(other)
    both = jnp.where(
        side == 0, jnp.concatenate([mine, got], axis=0), jnp.concatenate([got, mine], axis=0)
    )
    return both.T


def step(features, conv_weight, up_weight, cotangent):
    crops, frames, height, breadth, channels = features.shape
    rows = height * breadth
    times = lax.axis_size("tm")
    data = lax.axis_size("dp")
    scale = 1.0 / math.sqrt(crops * frames * rows * times * data)
    field = features.reshape(frames, rows, channels)
    cot = cotangent.reshape(2 * frames, rows, channels)
    side = (lax.axis_index("dp") % 2).astype(jnp.int32).reshape(1)
    block = (frames, rows, channels)
    square = 2 * channels * channels
    act = call(
        act_body,
        (frames,),
        [pl.BlockSpec((1, rows, channels), lambda f: (f, 0, 0))],
        pl.BlockSpec((1, rows, channels), lambda f: (f, 0, 0)),
        jax.ShapeDtypeStruct(block, BF16),
        flops=20 * frames * rows * channels,
        nbytes=4 * frames * rows * channels,
    )(field)
    act_prior = from_behind(act, "tm", 1)
    local, prior_part = call(
        up_body,
        (1,),
        [whole(*cot.shape), whole(*up_weight.shape)],
        [whole(*block), whole(*block)],
        [jax.ShapeDtypeStruct(block, F32), jax.ShapeDtypeStruct(block, BF16)],
        flops=6 * frames * rows * square,
        nbytes=10 * frames * rows * channels,
    )(cot, up_weight)
    next_part = from_behind(prior_part, "tm", -1)
    taps = conv_weight.reshape(27, channels, channels)
    turned = call(
        turn_body,
        (9,),
        [pl.BlockSpec((3, channels, channels), lambda n: (8 - n, 0, 0))],
        pl.BlockSpec((3, channels, channels), lambda n: (n, 0, 0)),
        jax.ShapeDtypeStruct(taps.shape, BF16),
        flops=27 * square,
        nbytes=4 * 27 * channels * channels,
    )(taps)
    turned = turned.reshape(3, 9 * channels, channels)
    conv_grad = (local + next_part.astype(F32)).astype(BF16)
    conv_next = from_behind(conv_grad, "tm", -1)
    columns = pltpu.VMEM((4 * rows, 9 * channels), BF16)
    sums = pltpu.VMEM((frames * rows, channels), F32)
    kernel_spec = pl.BlockSpec((1, 9 * channels, channels), lambda k: (k, 0, 0))
    act_prior, turned = lax.optimization_barrier((act_prior, turned))
    hidden = call(
        make_conv(breadth),
        (3,),
        [whole(*block), whole(*block), kernel_spec, whole(*block)],
        whole(*block),
        jax.ShapeDtypeStruct(block, BF16),
        [columns, sums],
        flops=27 * frames * rows * square,
        nbytes=2 * 27 * channels * channels,
    )(act_prior, act, conv_weight.reshape(3, 9 * channels, channels), field)
    hidden_prior = from_behind(hidden, "tm", 1)
    cut = channels // times // 2
    half = jax.ShapeDtypeStruct((times, cut, 27 * channels), BF16)
    half_spec = pl.BlockSpec((times, cut, 9 * channels), lambda k: (0, 0, k))
    send, keep = call(
        make_weight_grad(breadth, times),
        (3,),
        [pl.BlockSpec(memory_space=pltpu.SMEM), whole(*block), whole(*block), whole(*block)],
        [half_spec, half_spec],
        [half, half],
        [columns, pltpu.VMEM((channels, frames * rows), BF16)],
        flops=27 * frames * rows * square,
        nbytes=4 * 27 * channels * channels,
    )(side, act_prior, act, conv_grad)
    grad_conv = reduce_blocks(send, keep) * scale
    up_half = jax.ShapeDtypeStruct((times, channels // times, 3 * channels), BF16)
    up_send, up_keep = call(
        make_up_grad(times),
        (1,),
        [pl.BlockSpec(memory_space=pltpu.SMEM), whole(*block), whole(*block), whole(*cot.shape)],
        [whole(*up_half.shape), whole(*up_half.shape)],
        [up_half, up_half],
        [
            pltpu.VMEM((frames * rows, 3 * channels), BF16),
            pltpu.VMEM((2 * channels, frames * rows), BF16),
        ],
        flops=6 * frames * rows * square,
        nbytes=12 * channels * channels,
    )(side, hidden_prior, hidden, cot)
    grad_up = over_data(over_times(join_pair(up_send, up_keep))) * scale
    features_grad = call(
        make_back(breadth),
        (3,),
        [whole(*block), whole(*block), kernel_spec] + [whole(*block)] * 3,
        whole(*block),
        jax.ShapeDtypeStruct(block, BF16),
        [columns, sums],
        flops=27 * frames * rows * square,
        nbytes=2 * 27 * channels * channels,
    )(conv_grad, conv_next, turned, field, local, next_part)
    return (features_grad.reshape(features.shape), grad_conv, grad_up)


def solution(mesh):
    in_specs = (P("dp", "tm", None, None, None), P(), P(), P("dp", "tm", None, None, None))
    out_specs = (P("dp", "tm", None, None, None), P("dp", "tm"), P("dp", "tm"))
    return jax.shard_map(step, mesh=mesh, in_specs=in_specs, out_specs=out_specs, check_vma=False)
```

```python
import math

import jax
import jax.numpy as jnp
from jax import lax
from jax.experimental import pallas as pl
from jax.experimental.pallas import tpu as pltpu
from jax.sharding import PartitionSpec as P


G = 32
EPSILON = 1e-06
F32 = jnp.float32
BF16 = jnp.bfloat16
ROW_ROW = (((1,), (1,)), ((), ()))


def call(body, grid, ins, outs, shapes, scratch=(), flops=0, nbytes=0):
    return pl.pallas_call(
        body,
        grid=grid,
        in_specs=ins,
        out_specs=outs,
        out_shape=shapes,
        scratch_shapes=list(scratch),
        cost_estimate=pl.CostEstimate(flops=flops, bytes_accessed=nbytes, transcendentals=0),
        compiler_params=pltpu.CompilerParams(
            dimension_semantics=("arbitrary",) * len(grid), vmem_limit_bytes=56 * 2**20
        ),
    )


def whole(*shape):
    return pl.BlockSpec(shape, lambda *at: (0,) * len(shape))


def from_behind(value, axis, steps):
    count = lax.axis_size(axis)
    first, last = (max(0, -steps), min(count, count - steps))
    return lax.ppermute(value, axis, [(source, source + steps) for source in range(first, last)])


def group_means(values):
    rows, channels = values[0].shape
    width = channels // G
    slot = lax.broadcasted_iota(jnp.int32, (8, channels), 0)
    sums = jnp.zeros((8, channels), F32)
    for at, value in enumerate(values):
        sums = jnp.where(slot == at, jnp.sum(value, axis=0, keepdims=True), sums)
    left = lax.broadcasted_iota(jnp.int32, (channels, 1), 0) // width
    right = lax.broadcasted_iota(jnp.int32, (1, channels), 1) // width
    mix = jnp.where(left == right, 1.0, 0.0).astype(F32)
    total = jnp.dot(sums, mix, precision=lax.Precision.HIGHEST, preferred_element_type=F32)
    total = total * (1.0 / (rows * width))
    return [total[at : at + 1] for at in range(len(values))]


def normalize(values):
    centers = [value - mean for value, mean in zip(values, group_means(values))]
    spreads = group_means([center * center for center in centers])
    scales = [lax.rsqrt(spread + EPSILON) for spread in spreads]
    return [center * scale for center, scale in zip(centers, scales)], scales


def act_body(field_ref, act_ref):
    normed, _ = normalize([field_ref[frame].astype(F32) for frame in range(2)])
    for frame in range(2):
        act_ref[frame] = (normed[frame] / (1.0 + jnp.exp(-normed[frame]))).astype(BF16)


def up_body(cot_ref, weight_ref, local_ref, prior_ref):
    channels = cot_ref.shape[-1]
    weight = weight_ref[...]
    parts = []
    for frame in range(2):
        pair = jnp.concatenate([cot_ref[2 * frame], cot_ref[2 * frame + 1]], axis=1)
        parts.append(lax.dot_general(pair, weight, ROW_ROW, preferred_element_type=F32))
    first, second = parts
    low, mid, high = (slice(k * channels, (k + 1) * channels) for k in range(3))
    local_ref[0] = first[:, high] + second[:, mid]
    local_ref[1] = second[:, high]
    prior_ref[0] = first[:, low].astype(BF16)
    prior_ref[1] = (first[:, mid] + second[:, low]).astype(BF16)


def turn_body(weight_ref, out_ref):
    for tap in range(3):
        out_ref[tap] = weight_ref[2 - tap].astype(F32).T.astype(BF16)


def fill_shifts(frames, cols_ref, breadth):
    rows, channels = frames[0].shape
    wide = lax.broadcasted_iota(jnp.int32, (rows, 1), 0) % breadth
    for at, frame in enumerate(frames):
        value = frame.astype(F32)
        for wide_tap in range(3):
            moved = value
            if wide_tap != 1:
                moved = pltpu.roll(value, (1 - wide_tap) % rows, 0)
                edge = 0 if wide_tap == 0 else breadth - 1
                moved = moved * jnp.where(wide == edge, 0.0, 1.0).astype(F32)
            for high_tap in range(3):
                shifted = moved
                if high_tap == 0:
                    shifted = jnp.concatenate(
                        [jnp.zeros((breadth, channels), F32), moved[: rows - breadth]], axis=0
                    )
                elif high_tap == 2:
                    shifted = jnp.concatenate(
                        [moved[breadth:], jnp.zeros((breadth, channels), F32)], axis=0
                    )
                tap = high_tap * 3 + wide_tap
                cols_ref[at * rows : (at + 1) * rows, tap * channels : (tap + 1) * channels] = (
                    shifted.astype(BF16)
                )


def accumulate(step, weight_ref, cols_ref, acc_ref):
    rows = acc_ref.shape[0]
    part = jnp.dot(
        cols_ref[pl.ds(pl.multiple_of(step * (rows // 2), rows // 2), rows), :],
        weight_ref[0],
        preferred_element_type=F32,
    )

    @pl.when(step == 0)
    def _():
        acc_ref[...] = part

    @pl.when(step > 0)
    def _():
        acc_ref[...] += part


def make_conv(breadth):
    def body(early_ref, late_ref, weight_ref, field_ref, hidden_ref, cols_ref, acc_ref):
        step = pl.program_id(0)

        @pl.when(step == 0)
        def _():
            frames = [early_ref[0], early_ref[1], late_ref[0], late_ref[1]]
            fill_shifts(frames, cols_ref, breadth)

        accumulate(step, weight_ref, cols_ref, acc_ref)

        @pl.when(step == 2)
        def _():
            rows = acc_ref.shape[0] // 2
            for frame in range(2):
                total = field_ref[frame].astype(F32) + acc_ref[frame * rows : (frame + 1) * rows]
                hidden_ref[frame] = total.astype(BF16)

    return body


def make_back(breadth):
    def body(
        early_ref, late_ref, weight_ref, field_ref, local_ref, next_ref, out_ref, cols_ref, acc_ref
    ):
        step = pl.program_id(0)

        @pl.when(step == 0)
        def _():
            frames = [early_ref[0], early_ref[1], late_ref[0], late_ref[1]]
            fill_shifts(frames, cols_ref, breadth)

        accumulate(step, weight_ref, cols_ref, acc_ref)

        @pl.when(step == 2)
        def _():
            rows = acc_ref.shape[0] // 2
            normed, scales = normalize([field_ref[frame].astype(F32) for frame in range(2)])
            grads = []
            for frame in range(2):
                gate = 1.0 / (1.0 + jnp.exp(-normed[frame]))
                slope = gate * (1.0 + normed[frame] * (1.0 - gate))
                grads.append(acc_ref[frame * rows : (frame + 1) * rows] * slope)
            means = group_means(grads + [grads[frame] * normed[frame] for frame in range(2)])
            for frame in range(2):
                inner = grads[frame] - means[frame] - normed[frame] * means[2 + frame]
                hidden_grad = local_ref[frame] + next_ref[frame].astype(F32)
                out_ref[frame] = (hidden_grad + scales[frame] * inner).astype(BF16)

    return body


def split_store(part, side, send_ref, keep_ref, times, at):
    rows, width = part.shape
    halves = part.reshape(times, rows // times, width)
    low = halves[:, : rows // times // 2]
    high = halves[:, rows // times // 2 :]
    send_ref[:, :, at : at + width] = jnp.where(side == 0, high, low).astype(BF16)
    keep_ref[:, :, at : at + width] = jnp.where(side == 0, low, high).astype(BF16)


def make_weight_grad(breadth, times):
    def body(side_ref, early_ref, late_ref, grad_ref, send_ref, keep_ref, cols_ref, turned_ref):
        step = pl.program_id(0)
        rows, channels = early_ref.shape[1:]

        @pl.when(step == 0)
        def _():
            frames = [early_ref[0], early_ref[1], late_ref[0], late_ref[1]]
            fill_shifts(frames, cols_ref, breadth)
            for frame in range(2):
                turned_ref[:, frame * rows : (frame + 1) * rows] = (
                    grad_ref[frame].astype(F32).T.astype(BF16)
                )

        start = pl.multiple_of(step * rows, rows)
        turned = turned_ref[...]
        total = cols_ref.shape[1]
        for at in range(0, total, 2 * channels):
            width = min(2 * channels, total - at)
            part = jnp.dot(
                turned,
                cols_ref[pl.ds(start, 2 * rows), at : at + width],
                preferred_element_type=F32,
            )
            split_store(part, side_ref[0], send_ref, keep_ref, times, at)

    return body


def make_up_grad(times):
    def body(side_ref, early_ref, late_ref, cot_ref, send_ref, keep_ref, cols_ref, turned_ref):
        rows, channels = early_ref.shape[1:]
        frames = [early_ref[0], early_ref[1], late_ref[0], late_ref[1]]
        for tap in range(3):
            for frame in range(2):
                cols_ref[
                    frame * rows : (frame + 1) * rows, tap * channels : (tap + 1) * channels
                ] = frames[frame + tap]
        for frame in range(2):
            for half in range(2):
                turned_ref[
                    half * channels : (half + 1) * channels, frame * rows : (frame + 1) * rows
                ] = cot_ref[2 * frame + half].astype(F32).T.astype(BF16)
        part = jnp.dot(turned_ref[...], cols_ref[...], preferred_element_type=F32)
        split_store(part, side_ref[0], send_ref, keep_ref, times, 0)

    return body


def swap_sides(value):
    return lax.ppermute(value, "dp", [(d, d ^ 1) for d in range(lax.axis_size("dp"))])


def place_of(device):
    time, data = divmod(device, 16)
    return [data // 4, time // 2, (data // 2 % 2) * 2 + time % 2, data % 2]


def device_at(x, y, z, core):
    return (y * 2 + z % 2) * 16 + x * 4 + z // 2 * 2 + core


def exchange(pieces, ring):
    got = [pieces[0]]
    for step in (1, 2, 3):
        pairs = []
        for device in range(128):
            place = place_of(device)
            place[ring] = (place[ring] + step) % 4
            pairs.append((device, device_at(*place)))
        got.append(lax.ppermute(pieces[step], ("tm", "dp"), pairs))
    return got


def added(refs):
    total = refs[0][...].astype(F32)
    for ref in refs[1:]:
        total = total + ref[...].astype(F32)
    return total


def pick(value, widths, index, count):
    parts, start = [], 0
    for width in widths:
        part = width // count
        parts.append(value[:, start + index * part : start + (index + 1) * part])
        start += width
    return jnp.concatenate(parts, axis=1)


def make_join(conv_rows, up_rows):
    widths = (conv_rows, up_rows, up_rows)

    def body(place_ref, conv_got, conv_keep, up_got, up_keep, *refs):
        row_refs, col_refs, hold_ref = refs[:4], refs[4:8], refs[8]
        step = pl.program_id(0)
        conv = conv_got[0] + conv_keep[0]
        up = up_got[0] + up_keep[0]
        cols = conv.shape[1]
        full = [
            jnp.concatenate([conv[low], up[low, :cols], up[low, cols:]], axis=1)
            for low in range(2)
        ]
        for at in range(4):
            hold_ref[at] = pick(full[0], widths, at, 4)
        for slot in range(4):
            row_refs[slot][0] = hold_ref[lax.rem(place_ref[0] + slot, 4)]

            @pl.when(lax.rem(step - place_ref[1] + 4, 4) == slot)
            def _():
                col_refs[slot][...] = full[1]

    return body


def make_mid(conv_rows, up_rows):
    widths = (conv_rows, up_rows, up_rows)

    def body(place_ref, *refs):
        row_in, col_in, row_out, col_out = refs[:4], refs[4:8], refs[8:12], refs[12:16]
        row_hold, col_hold = refs[16:]
        row_hold[...] = added(row_in)
        total = added(col_in)
        for at in range(4):
            col_hold[at] = pick(total, widths, at, 4)
        for slot in range(4):
            kind = row_out[slot].dtype
            row_out[slot][...] = row_hold[lax.rem(place_ref[1] + slot, 4)].astype(kind)
            col_out[slot][...] = col_hold[lax.rem(place_ref[0] + slot, 4)].astype(kind)

    return body


def make_end(conv_rows, up_rows):
    widths = (conv_rows // 4, up_rows // 4, up_rows // 4)

    def body(place_ref, *refs):
        outs, hold_ref = refs[8:12], refs[12]
        for low in range(2):
            total = added(refs[4 * low : 4 * low + 4])
            for high in range(2):
                hold_ref[high * 2 + low] = pick(total, widths, high, 2)
        for slot in range(4):
            outs[slot][...] = hold_ref[lax.rem(place_ref[2] + slot, 4)].astype(outs[slot].dtype)

    return body


def make_last(conv_rows, up_rows):
    widths = (conv_rows // 8, up_rows // 8, up_rows // 8)

    def body(place_ref, *refs):
        total = added(refs[:4])
        low, high = pick(total, widths, 0, 2), pick(total, widths, 1, 2)
        refs[4][...] = jnp.where(place_ref[3] == 0, low, high)
        refs[5][...] = jnp.where(place_ref[3] == 0, high, low)

    return body


def reduce_blocks(conv_send, conv_keep, up_send, up_keep):
    times, cols, conv_rows = conv_send.shape
    up_rows = up_send.shape[2]
    rows = conv_rows + 2 * up_rows
    data, time = lax.axis_index("dp"), lax.axis_index("tm")
    place = jnp.stack([data // 4, time // 2, (data // 2 % 2) * 2 + time % 2, data % 2])
    place = place.astype(jnp.int32)
    scalars = pl.BlockSpec(memory_space=pltpu.SMEM)

    def small(make, arrays, shapes, scratch):
        return call(
            make(conv_rows, up_rows),
            (1,),
            [scalars] + [whole(*array.shape) for array in arrays],
            [whole(*shape.shape) for shape in shapes],
            shapes,
            scratch,
            flops=1000,
            nbytes=2 * times * cols * rows,
        )(place, *arrays)

    def shape(*dims):
        return jax.ShapeDtypeStruct(dims, BF16)

    def slots(*dims):
        return [jax.ShapeDtypeStruct(dims, F32)] + [jax.ShapeDtypeStruct(dims, BF16)] * 3

    conv_got = swap_sides(conv_send)
    up_got = swap_sides(up_send)
    conv_blocks = (4, 2, cols, conv_rows)
    up_blocks = (4, 2, 2 * cols, up_rows)
    conv_spec = pl.BlockSpec((1,) + conv_blocks[1:], lambda k: (k, 0, 0, 0))
    up_spec = pl.BlockSpec((1,) + up_blocks[1:], lambda k: (k, 0, 0, 0))
    row_spec = pl.BlockSpec((1, cols, rows // 4), lambda k: (k, 0, 0))
    out = call(
        make_join(conv_rows, up_rows),
        (4,),
        [scalars, conv_spec, conv_spec, up_spec, up_spec],
        [row_spec] * 4 + [whole(cols, rows)] * 4,
        [shape(4, cols, rows // 4)] * 4 + [shape(cols, rows)] * 4,
        [pltpu.VMEM((4, cols, rows // 4), BF16)],
        flops=1000,
        nbytes=6 * times * cols * rows,
    )(
        place,
        conv_got.reshape(conv_blocks),
        conv_keep.reshape(conv_blocks),
        up_got.reshape(up_blocks),
        up_keep.reshape(up_blocks),
    )
    first = exchange(out[4:], 1)
    second = exchange(out[:4], 0)
    hold = pltpu.VMEM((4, cols, rows // 4), F32)
    out = small(make_mid, second + first, slots(cols, rows // 4) * 2, [hold, hold])
    first = exchange(out[:4], 1)
    second = exchange(out[4:], 0)
    hold = pltpu.VMEM((4, cols, rows // 8), F32)
    out = small(make_end, first + second, slots(cols, rows // 8), [hold])
    out = exchange(out, 2)
    half = jax.ShapeDtypeStruct((cols, rows // 16), F32)
    mine, other = small(make_last, out, [half, half], [])
    got = swap_sides(other)
    even = data % 2 == 0
    low, high = jnp.where(even, mine, got), jnp.where(even, got, mine)
    cut, part = conv_rows // 16, up_rows // 16
    grad_conv = jnp.concatenate([low[:, :cut], high[:, :cut]], axis=0).T
    grad_up = jnp.concatenate(
        [
            side[:, cut + at * part : cut + (at + 1) * part]
            for side in (low, high)
            for at in range(2)
        ],
        axis=0,
    ).T
    return grad_conv, grad_up


def step(features, conv_weight, up_weight, cotangent):
    crops, frames, height, breadth, channels = features.shape
    rows = height * breadth
    times = lax.axis_size("tm")
    data = lax.axis_size("dp")
    scale = 1.0 / math.sqrt(crops * frames * rows * times * data)
    field = features.reshape(frames, rows, channels)
    cot = cotangent.reshape(2 * frames, rows, channels)
    side = (lax.axis_index("dp") % 2).astype(jnp.int32).reshape(1)
    block = (frames, rows, channels)
    square = 2 * channels * channels
    act = call(
        act_body,
        (1,),
        [whole(*block)],
        whole(*block),
        jax.ShapeDtypeStruct(block, BF16),
        flops=20 * frames * rows * channels,
        nbytes=4 * frames * rows * channels,
    )(field)
    act_prior = from_behind(act, "tm", 1)
    local, prior_part = call(
        up_body,
        (1,),
        [whole(*cot.shape), whole(*up_weight.shape)],
        [whole(*block), whole(*block)],
        [jax.ShapeDtypeStruct(block, F32), jax.ShapeDtypeStruct(block, BF16)],
        flops=6 * frames * rows * square,
        nbytes=10 * frames * rows * channels,
    )(cot, up_weight)
    next_part = from_behind(prior_part, "tm", -1)
    taps = conv_weight.reshape(27, channels, channels)
    turned = call(
        turn_body,
        (9,),
        [pl.BlockSpec((3, channels, channels), lambda n: (8 - n, 0, 0))],
        pl.BlockSpec((3, channels, channels), lambda n: (n, 0, 0)),
        jax.ShapeDtypeStruct(taps.shape, BF16),
        flops=27 * square,
        nbytes=4 * 27 * channels * channels,
    )(taps)
    turned = turned.reshape(3, 9 * channels, channels)
    conv_grad = (local + next_part.astype(F32)).astype(BF16)
    conv_next = from_behind(conv_grad, "tm", -1)
    columns = pltpu.VMEM((4 * rows, 9 * channels), BF16)
    sums = pltpu.VMEM((frames * rows, channels), F32)
    kernel_spec = pl.BlockSpec((1, 9 * channels, channels), lambda k: (k, 0, 0))
    act_prior, turned = lax.optimization_barrier((act_prior, turned))
    hidden = call(
        make_conv(breadth),
        (3,),
        [whole(*block), whole(*block), kernel_spec, whole(*block)],
        whole(*block),
        jax.ShapeDtypeStruct(block, BF16),
        [columns, sums],
        flops=27 * frames * rows * square,
        nbytes=2 * 27 * channels * channels,
    )(act_prior, act, conv_weight.reshape(3, 9 * channels, channels), field)
    hidden_prior = from_behind(hidden, "tm", 1)
    cut = channels // times // 2
    half = jax.ShapeDtypeStruct((times, cut, 27 * channels), BF16)
    half_spec = pl.BlockSpec((times, cut, 9 * channels), lambda k: (0, 0, k))
    send, keep = call(
        make_weight_grad(breadth, times),
        (3,),
        [pl.BlockSpec(memory_space=pltpu.SMEM), whole(*block), whole(*block), whole(*block)],
        [half_spec, half_spec],
        [half, half],
        [columns, pltpu.VMEM((channels, frames * rows), BF16)],
        flops=27 * frames * rows * square,
        nbytes=4 * 27 * channels * channels,
    )(side, act_prior, act, conv_grad)
    up_half = jax.ShapeDtypeStruct((times, channels // times, 3 * channels), BF16)
    up_send, up_keep = call(
        make_up_grad(times),
        (1,),
        [pl.BlockSpec(memory_space=pltpu.SMEM), whole(*block), whole(*block), whole(*cot.shape)],
        [whole(*up_half.shape), whole(*up_half.shape)],
        [up_half, up_half],
        [
            pltpu.VMEM((frames * rows, 3 * channels), BF16),
            pltpu.VMEM((2 * channels, frames * rows), BF16),
        ],
        flops=6 * frames * rows * square,
        nbytes=12 * channels * channels,
    )(side, hidden_prior, hidden, cot)
    grad_conv, grad_up = reduce_blocks(send, keep, up_send, up_keep)
    grad_conv, grad_up = grad_conv * scale, grad_up * scale
    features_grad = call(
        make_back(breadth),
        (3,),
        [whole(*block), whole(*block), kernel_spec] + [whole(*block)] * 3,
        whole(*block),
        jax.ShapeDtypeStruct(block, BF16),
        [columns, sums],
        flops=27 * frames * rows * square,
        nbytes=2 * 27 * channels * channels,
    )(conv_grad, conv_next, turned, field, local, next_part)
    return (features_grad.reshape(features.shape), grad_conv, grad_up)


def solution(mesh):
    in_specs = (P("dp", "tm", None, None, None), P(), P(), P("dp", "tm", None, None, None))
    out_specs = (P("dp", "tm", None, None, None), P("dp", "tm"), P("dp", "tm"))
    return jax.shard_map(step, mesh=mesh, in_specs=in_specs, out_specs=out_specs, check_vma=False)
```

```python
import math

import jax
import jax.numpy as jnp
from jax import lax
from jax.experimental import pallas as pl
from jax.experimental.pallas import tpu as pltpu
from jax.sharding import PartitionSpec as P


G = 32
EPSILON = 1e-06
F32 = jnp.float32
BF16 = jnp.bfloat16
ROW_ROW = (((1,), (1,)), ((), ()))

LIMIT = 23 * 2**20


def call(body, grid, ins, outs, shapes, scratch=(), flops=0, nbytes=0):
    return pl.pallas_call(
        body,
        grid=grid,
        in_specs=ins,
        out_specs=outs,
        out_shape=shapes,
        scratch_shapes=list(scratch),
        cost_estimate=pl.CostEstimate(flops=flops, bytes_accessed=nbytes, transcendentals=0),
        compiler_params=pltpu.CompilerParams(
            dimension_semantics=("arbitrary",) * len(grid), vmem_limit_bytes=LIMIT
        ),
    )


def whole(*shape):
    return pl.BlockSpec(shape, lambda *at: (0,) * len(shape), pipeline_mode=pl.Buffered(1))


RESIDENT = pl.BlockSpec(memory_space=pltpu.VMEM)


def from_behind(value, axis, steps):
    count = lax.axis_size(axis)
    first, last = (max(0, -steps), min(count, count - steps))
    return lax.ppermute(value, axis, [(source, source + steps) for source in range(first, last)])


def own_place():
    data, time = lax.axis_index("dp"), lax.axis_index("tm")
    core = lax.rem(data, 2)
    high = lax.rem(lax.div(data, 2), 2)
    return lax.div(data, 4), lax.div(time, 2), high * 2 + lax.rem(time, 2), core


def group_means(values):
    rows, channels = values[0].shape
    width = channels // G
    slot = lax.broadcasted_iota(jnp.int32, (8, channels), 0)
    sums = jnp.zeros((8, channels), F32)
    for at, value in enumerate(values):
        sums = jnp.where(slot == at, jnp.sum(value, axis=0, keepdims=True), sums)
    left = lax.broadcasted_iota(jnp.int32, (channels, 1), 0) // width
    right = lax.broadcasted_iota(jnp.int32, (1, channels), 1) // width
    mix = jnp.where(left == right, 1.0, 0.0).astype(F32)
    total = jnp.dot(sums, mix, precision=lax.Precision.HIGHEST, preferred_element_type=F32)
    total = total * (1.0 / (rows * width))
    return [total[at : at + 1] for at in range(len(values))]


def normalize(values):
    centers = [value - mean for value, mean in zip(values, group_means(values))]
    spreads = group_means([center * center for center in centers])
    scales = [lax.rsqrt(spread + EPSILON) for spread in spreads]
    return [center * scale for center, scale in zip(centers, scales)], scales


def act_body(field_ref, act_ref):
    normed, _ = normalize([field_ref[frame].astype(F32) for frame in range(2)])
    for frame in range(2):
        act_ref[frame] = (normed[frame] / (1.0 + jnp.exp(-normed[frame]))).astype(BF16)


def up_body(cot_ref, weight_ref, ahead_ref, local_ref, prior_ref):
    channels = cot_ref.shape[-1]
    weight = weight_ref[...]
    parts = []
    for frame in range(2):
        pair = jnp.concatenate([cot_ref[2 * frame], cot_ref[2 * frame + 1]], axis=1)
        parts.append(lax.dot_general(pair, weight, ROW_ROW, preferred_element_type=F32))
    first, second = parts
    low, mid, high = (slice(k * channels, (k + 1) * channels) for k in range(3))
    local_ref[0] = first[:, high] + second[:, mid]
    local_ref[1] = second[:, high]
    prior_ref[0] = first[:, low].astype(BF16)
    prior_ref[1] = (first[:, mid] + second[:, low]).astype(BF16)


def turn_body(weight_ref, out_ref):
    step = pl.program_id(0)
    for tap in range(3):
        at = step * 3 + tap
        out_ref[at] = weight_ref[26 - at].astype(F32).T.astype(BF16)


def fill_shifts(frames, cols_ref, breadth):
    rows, channels = frames[0].shape
    wide = lax.broadcasted_iota(jnp.int32, (rows, 1), 0) % breadth
    for at, frame in enumerate(frames):
        value = frame.astype(F32)
        for wide_tap in range(3):
            moved = value
            if wide_tap != 1:
                moved = pltpu.roll(value, (1 - wide_tap) % rows, 0)
                edge = 0 if wide_tap == 0 else breadth - 1
                moved = moved * jnp.where(wide == edge, 0.0, 1.0).astype(F32)
            for high_tap in range(3):
                shifted = moved
                if high_tap == 0:
                    shifted = jnp.concatenate(
                        [jnp.zeros((breadth, channels), F32), moved[: rows - breadth]], axis=0
                    )
                elif high_tap == 2:
                    shifted = jnp.concatenate(
                        [moved[breadth:], jnp.zeros((breadth, channels), F32)], axis=0
                    )
                tap = high_tap * 3 + wide_tap
                cols_ref[at * rows : (at + 1) * rows, tap * channels : (tap + 1) * channels] = (
                    shifted.astype(BF16)
                )


def accumulate(step, weight_ref, cols_ref, acc_ref):
    rows = acc_ref.shape[0]
    part = jnp.dot(
        cols_ref[pl.ds(pl.multiple_of(step * (rows // 2), rows // 2), rows), :],
        weight_ref[step],
        preferred_element_type=F32,
    )

    @pl.when(step == 0)
    def _():
        acc_ref[...] = part

    @pl.when(step > 0)
    def _():
        acc_ref[...] += part


def make_conv(breadth):
    def body(early_ref, late_ref, weight_ref, field_ref, hidden_ref, cols_ref, acc_ref):
        step = pl.program_id(0)

        @pl.when(step == 0)
        def _():
            frames = [early_ref[0], early_ref[1], late_ref[0], late_ref[1]]
            fill_shifts(frames, cols_ref, breadth)

        accumulate(step, weight_ref, cols_ref, acc_ref)

        @pl.when(step == 2)
        def _():
            rows = acc_ref.shape[0] // 2
            for frame in range(2):
                total = field_ref[frame].astype(F32) + acc_ref[frame * rows : (frame + 1) * rows]
                hidden_ref[frame] = total.astype(BF16)

    return body


def make_back(breadth):
    def body(
        early_ref, late_ref, weight_ref, field_ref, local_ref, next_ref, out_ref, cols_ref, acc_ref
    ):
        step = pl.program_id(0)

        @pl.when(step == 0)
        def _():
            frames = [early_ref[0], early_ref[1], late_ref[0], late_ref[1]]
            fill_shifts(frames, cols_ref, breadth)

        accumulate(step, weight_ref, cols_ref, acc_ref)

        @pl.when(step == 2)
        def _():
            rows = acc_ref.shape[0] // 2
            normed, scales = normalize([field_ref[frame].astype(F32) for frame in range(2)])
            grads = []
            for frame in range(2):
                gate = 1.0 / (1.0 + jnp.exp(-normed[frame]))
                slope = gate * (1.0 + normed[frame] * (1.0 - gate))
                grads.append(acc_ref[frame * rows : (frame + 1) * rows] * slope)
            means = group_means(grads + [grads[frame] * normed[frame] for frame in range(2)])
            for frame in range(2):
                inner = grads[frame] - means[frame] - normed[frame] * means[2 + frame]
                hidden_grad = local_ref[frame] + next_ref[frame].astype(F32)
                out_ref[frame] = (hidden_grad + scales[frame] * inner).astype(BF16)

    return body


def split_store(part, side, send_ref, keep_ref, times, at):
    rows, width = part.shape
    halves = part.reshape(times, rows // times, width)
    low = halves[:, : rows // times // 2]
    high = halves[:, rows // times // 2 :]
    send_ref[:, :, at : at + width] = jnp.where(side == 0, high, low).astype(BF16)
    keep_ref[:, :, at : at + width] = jnp.where(side == 0, low, high).astype(BF16)


def make_weight_grad(breadth, times):
    def body(early_ref, late_ref, grad_ref, send_ref, keep_ref, cols_ref, turned_ref):
        step = pl.program_id(0)
        rows, channels = early_ref.shape[1:]

        @pl.when(step == 0)
        def _():
            frames = [early_ref[0], early_ref[1], late_ref[0], late_ref[1]]
            fill_shifts(frames, cols_ref, breadth)
            for frame in range(2):
                turned_ref[:, frame * rows : (frame + 1) * rows] = (
                    grad_ref[frame].astype(F32).T.astype(BF16)
                )

        start = pl.multiple_of(step * rows, rows)
        turned = turned_ref[...]
        total = cols_ref.shape[1]
        for at in range(0, total, 2 * channels):
            width = min(2 * channels, total - at)
            part = jnp.dot(
                turned,
                cols_ref[pl.ds(start, 2 * rows), at : at + width],
                preferred_element_type=F32,
            )
            split_store(part, own_place()[3], send_ref, keep_ref, times, at)

    return body


def make_up_grad(times):
    def body(early_ref, late_ref, cot_ref, send_ref, keep_ref, cols_ref, turned_ref):
        rows, channels = early_ref.shape[1:]
        frames = [early_ref[0], early_ref[1], late_ref[0], late_ref[1]]
        for tap in range(3):
            for frame in range(2):
                cols_ref[
                    frame * rows : (frame + 1) * rows, tap * channels : (tap + 1) * channels
                ] = frames[frame + tap]
        for frame in range(2):
            for half in range(2):
                turned_ref[
                    half * channels : (half + 1) * channels, frame * rows : (frame + 1) * rows
                ] = cot_ref[2 * frame + half].astype(F32).T.astype(BF16)
        part = jnp.dot(turned_ref[...], cols_ref[...], preferred_element_type=F32)
        split_store(part, own_place()[3], send_ref, keep_ref, times, 0)

    return body


def swap_sides(value):
    return lax.ppermute(value, "dp", [(d, d ^ 1) for d in range(lax.axis_size("dp"))])


def place_of(device):
    time, data = divmod(device, 16)
    return [data // 4, time // 2, (data // 2 % 2) * 2 + time % 2, data % 2]


def device_at(x, y, z, core):
    return (y * 2 + z % 2) * 16 + x * 4 + z // 2 * 2 + core


def exchange(pieces, ring):
    got = [pieces[0]]
    for step in (1, 2, 3):
        pairs = []
        for device in range(128):
            place = place_of(device)
            place[ring] = (place[ring] + step) % 4
            pairs.append((device, device_at(*place)))
        got.append(lax.ppermute(pieces[step], ("tm", "dp"), pairs))
    return got


def added(refs):
    total = refs[0][...].astype(F32)
    for ref in refs[1:]:
        total = total + ref[...].astype(F32)
    return total


def pick(value, widths, index, count):
    parts, start = [], 0
    for width in widths:
        part = width // count
        parts.append(value[:, start + index * part : start + (index + 1) * part])
        start += width
    return jnp.concatenate(parts, axis=1)


def make_join(conv_rows, up_rows):
    widths = (conv_rows, up_rows, up_rows)

    def body(conv_got, conv_keep, up_got, up_keep, *refs):
        row_refs, col_refs, hold_ref = refs[:4], refs[4:8], refs[8]
        step = pl.program_id(0)
        conv = conv_got[0] + conv_keep[0]
        up = up_got[0] + up_keep[0]
        cols = conv.shape[1]
        full = [
            jnp.concatenate([conv[low], up[low, :cols], up[low, cols:]], axis=1)
            for low in range(2)
        ]
        for at in range(4):
            hold_ref[at] = pick(full[0], widths, at, 4)
        for slot in range(4):
            row_refs[slot][0] = hold_ref[lax.rem(own_place()[0] + slot, 4)]

            @pl.when(lax.rem(step - own_place()[1] + 4, 4) == slot)
            def _():
                col_refs[slot][...] = full[1]

    return body


def make_mid(conv_rows, up_rows):
    widths = (conv_rows, up_rows, up_rows)

    def body(*refs):
        row_in, col_in, row_out, col_out = refs[:4], refs[4:8], refs[8:12], refs[12:16]
        row_hold, col_hold = refs[16:]
        row_hold[...] = added(row_in)
        total = added(col_in)
        for at in range(4):
            col_hold[at] = pick(total, widths, at, 4)
        for slot in range(4):
            kind = row_out[slot].dtype
            row_out[slot][...] = row_hold[lax.rem(own_place()[1] + slot, 4)].astype(kind)
            col_out[slot][...] = col_hold[lax.rem(own_place()[0] + slot, 4)].astype(kind)

    return body


def make_end(conv_rows, up_rows):
    widths = (conv_rows // 4, up_rows // 4, up_rows // 4)

    def body(*refs):
        outs, hold_ref = refs[8:12], refs[12]
        for low in range(2):
            total = added(refs[4 * low : 4 * low + 4])
            for high in range(2):
                hold_ref[high * 2 + low] = pick(total, widths, high, 2)
        for slot in range(4):
            outs[slot][...] = hold_ref[lax.rem(own_place()[2] + slot, 4)].astype(outs[slot].dtype)

    return body


def make_last(conv_rows, up_rows):
    widths = (conv_rows // 8, up_rows // 8, up_rows // 8)

    def body(*refs):
        total = added(refs[:4])
        low, high = pick(total, widths, 0, 2), pick(total, widths, 1, 2)
        refs[4][...] = jnp.where(own_place()[3] == 0, low, high)
        refs[5][...] = jnp.where(own_place()[3] == 0, high, low)

    return body


def make_spread(conv_rows, up_rows, scale):
    cut, part = conv_rows // 16, up_rows // 16

    def body(mine_ref, got_ref, conv_ref, up_ref):
        even = own_place()[3] == 0
        mine, got = mine_ref[...], got_ref[...]
        sides = jnp.where(even, mine, got), jnp.where(even, got, mine)
        conv_ref[...] = jnp.concatenate([side[:, :cut] for side in sides], axis=0).T * scale
        pieces = [
            side[:, cut + at * part : cut + (at + 1) * part] for side in sides for at in range(2)
        ]
        up_ref[...] = jnp.concatenate(pieces, axis=0).T * scale

    return body


def reduce_blocks(conv_send, conv_keep, up_send, up_keep, scale):
    times, cols, conv_rows = conv_send.shape
    up_rows = up_send.shape[2]
    rows = conv_rows + 2 * up_rows

    def small(make, arrays, shapes, scratch):
        return call(
            make(conv_rows, up_rows),
            (1,),
            [whole(*array.shape) for array in arrays],
            [whole(*shape.shape) for shape in shapes],
            shapes,
            scratch,
            flops=1000,
            nbytes=2 * times * cols * rows,
        )(*arrays)

    def shape(*dims):
        return jax.ShapeDtypeStruct(dims, BF16)

    def slots(*dims):
        return [jax.ShapeDtypeStruct(dims, F32)] + [jax.ShapeDtypeStruct(dims, BF16)] * 3

    conv_got = swap_sides(conv_send)
    up_got = swap_sides(up_send)
    conv_blocks = (4, 2, cols, conv_rows)
    up_blocks = (4, 2, 2 * cols, up_rows)
    conv_spec = pl.BlockSpec((1,) + conv_blocks[1:], lambda k: (k, 0, 0, 0))
    up_spec = pl.BlockSpec((1,) + up_blocks[1:], lambda k: (k, 0, 0, 0))
    row_spec = pl.BlockSpec((1, cols, rows // 4), lambda k: (k, 0, 0))
    out = call(
        make_join(conv_rows, up_rows),
        (4,),
        [conv_spec, conv_spec, up_spec, up_spec],
        [row_spec] * 4 + [whole(cols, rows)] * 4,
        [shape(4, cols, rows // 4)] * 4 + [shape(cols, rows)] * 4,
        [pltpu.VMEM((4, cols, rows // 4), BF16)],
        flops=1000,
        nbytes=6 * times * cols * rows,
    )(
        conv_got.reshape(conv_blocks),
        conv_keep.reshape(conv_blocks),
        up_got.reshape(up_blocks),
        up_keep.reshape(up_blocks),
    )
    first = exchange(out[4:], 1)
    second = exchange(out[:4], 0)
    hold = pltpu.VMEM((4, cols, rows // 4), F32)
    out = small(make_mid, second + first, slots(cols, rows // 4) * 2, [hold, hold])
    first = exchange(out[:4], 1)
    second = exchange(out[4:], 0)
    hold = pltpu.VMEM((4, cols, rows // 8), F32)
    out = small(make_end, first + second, slots(cols, rows // 8), [hold])
    out = exchange(out, 2)
    half = jax.ShapeDtypeStruct((cols, rows // 16), F32)
    mine, other = small(make_last, out, [half, half], [])
    got = swap_sides(other)
    cut, part = conv_rows // 16, up_rows // 16
    return small(
        lambda *sizes: make_spread(*sizes, scale),
        [mine, got],
        [
            jax.ShapeDtypeStruct((cut, 2 * cols), F32),
            jax.ShapeDtypeStruct((part, 4 * cols), F32),
        ],
        [],
    )


def step(features, conv_weight, up_weight, cotangent):
    crops, frames, height, breadth, channels = features.shape
    rows = height * breadth
    times = lax.axis_size("tm")
    data = lax.axis_size("dp")
    scale = 1.0 / math.sqrt(crops * frames * rows * times * data)
    field = features.reshape(frames, rows, channels)
    cot = cotangent.reshape(2 * frames, rows, channels)
    block = (frames, rows, channels)
    square = 2 * channels * channels
    act = call(
        act_body,
        (1,),
        [whole(*block)],
        whole(*block),
        jax.ShapeDtypeStruct(block, BF16),
        flops=20 * frames * rows * channels,
        nbytes=4 * frames * rows * channels,
    )(field)
    act_prior = from_behind(act, "tm", 1)
    local, prior_part = call(
        up_body,
        (1,),
        [whole(*cot.shape), whole(*up_weight.shape), RESIDENT],
        [whole(*block), whole(*block)],
        [jax.ShapeDtypeStruct(block, F32), jax.ShapeDtypeStruct(block, BF16)],
        flops=6 * frames * rows * square,
        nbytes=10 * frames * rows * channels,
    )(cot, up_weight, conv_weight)
    next_part = from_behind(prior_part, "tm", -1)
    taps = conv_weight.reshape(27, channels, channels)
    turned = call(
        turn_body,
        (9,),
        [RESIDENT],
        RESIDENT,
        jax.ShapeDtypeStruct(taps.shape, BF16),
        flops=27 * square,
        nbytes=4 * 27 * channels * channels,
    )(taps)
    turned = turned.reshape(3, 9 * channels, channels)
    conv_grad = (local + next_part.astype(F32)).astype(BF16)
    conv_next = from_behind(conv_grad, "tm", -1)
    columns = pltpu.VMEM((4 * rows, 9 * channels), BF16)
    sums = pltpu.VMEM((frames * rows, channels), F32)
    hidden = call(
        make_conv(breadth),
        (3,),
        [whole(*block), whole(*block), RESIDENT, whole(*block)],
        whole(*block),
        jax.ShapeDtypeStruct(block, BF16),
        [columns, sums],
        flops=27 * frames * rows * square,
        nbytes=2 * 27 * channels * channels,
    )(act_prior, act, conv_weight.reshape(3, 9 * channels, channels), field)
    hidden_prior = from_behind(hidden, "tm", 1)
    cut = channels // times // 2
    half = jax.ShapeDtypeStruct((times, cut, 27 * channels), BF16)
    half_spec = pl.BlockSpec((times, cut, 9 * channels), lambda k: (0, 0, k))
    send, keep = call(
        make_weight_grad(breadth, times),
        (3,),
        [whole(*block), whole(*block), whole(*block)],
        [half_spec, half_spec],
        [half, half],
        [columns, pltpu.VMEM((channels, frames * rows), BF16)],
        flops=27 * frames * rows * square,
        nbytes=4 * 27 * channels * channels,
    )(act_prior, act, conv_grad)
    up_half = jax.ShapeDtypeStruct((times, channels // times, 3 * channels), BF16)
    up_send, up_keep = call(
        make_up_grad(times),
        (1,),
        [whole(*block), whole(*block), whole(*cot.shape)],
        [whole(*up_half.shape), whole(*up_half.shape)],
        [up_half, up_half],
        [
            pltpu.VMEM((frames * rows, 3 * channels), BF16),
            pltpu.VMEM((2 * channels, frames * rows), BF16),
        ],
        flops=6 * frames * rows * square,
        nbytes=12 * channels * channels,
    )(hidden_prior, hidden, cot)
    grad_conv, grad_up = reduce_blocks(send, keep, up_send, up_keep, scale)
    features_grad = call(
        make_back(breadth),
        (3,),
        [whole(*block), whole(*block), RESIDENT] + [whole(*block)] * 3,
        whole(*block),
        jax.ShapeDtypeStruct(block, BF16),
        [columns, sums],
        flops=27 * frames * rows * square,
        nbytes=2 * 27 * channels * channels,
    )(conv_grad, conv_next, turned, field, local, next_part)
    return (features_grad.reshape(features.shape), grad_conv, grad_up)


def solution(mesh):
    in_specs = (P("dp", "tm", None, None, None), P(), P(), P("dp", "tm", None, None, None))
    out_specs = (P("dp", "tm", None, None, None), P("dp", "tm"), P("dp", "tm"))
    return jax.shard_map(step, mesh=mesh, in_specs=in_specs, out_specs=out_specs, check_vma=False)
```

```python
import math

import jax
import jax.numpy as jnp
from jax import lax
from jax.experimental import pallas as pl
from jax.experimental.pallas import tpu as pltpu
from jax.sharding import PartitionSpec as P


G = 32
EPSILON = 1e-06
F32 = jnp.float32
BF16 = jnp.bfloat16
ROW_ROW = (((1,), (1,)), ((), ()))

LIMIT = 23 * 2**20


def call(body, grid, ins, outs, shapes, scratch=(), flops=0, nbytes=0):
    return pl.pallas_call(
        body,
        grid=grid,
        in_specs=ins,
        out_specs=outs,
        out_shape=shapes,
        scratch_shapes=list(scratch),
        cost_estimate=pl.CostEstimate(flops=flops, bytes_accessed=nbytes, transcendentals=0),
        compiler_params=pltpu.CompilerParams(
            dimension_semantics=("arbitrary",) * len(grid), vmem_limit_bytes=LIMIT
        ),
    )


def whole(*shape):
    return pl.BlockSpec(shape, lambda *at: (0,) * len(shape), pipeline_mode=pl.Buffered(1))


RESIDENT = pl.BlockSpec(memory_space=pltpu.VMEM)


def from_behind(value, axis, steps):
    count = lax.axis_size(axis)
    first, last = (max(0, -steps), min(count, count - steps))
    return lax.ppermute(value, axis, [(source, source + steps) for source in range(first, last)])


def own_place():
    data, time = lax.axis_index("dp"), lax.axis_index("tm")
    core = lax.rem(data, 2)
    high = lax.rem(lax.div(data, 2), 2)
    return lax.div(data, 4), lax.div(time, 2), high * 2 + lax.rem(time, 2), core


def group_means(values):
    rows, channels = values[0].shape
    width = channels // G
    slot = lax.broadcasted_iota(jnp.int32, (8, channels), 0)
    sums = jnp.zeros((8, channels), F32)
    for at, value in enumerate(values):
        sums = jnp.where(slot == at, jnp.sum(value, axis=0, keepdims=True), sums)
    left = lax.broadcasted_iota(jnp.int32, (channels, 1), 0) // width
    right = lax.broadcasted_iota(jnp.int32, (1, channels), 1) // width
    mix = jnp.where(left == right, 1.0, 0.0).astype(F32)
    total = jnp.dot(sums, mix, precision=lax.Precision.HIGHEST, preferred_element_type=F32)
    total = total * (1.0 / (rows * width))
    return [total[at : at + 1] for at in range(len(values))]


def normalize(values):
    centers = [value - mean for value, mean in zip(values, group_means(values))]
    spreads = group_means([center * center for center in centers])
    scales = [lax.rsqrt(spread + EPSILON) for spread in spreads]
    return [center * scale for center, scale in zip(centers, scales)], scales


def act_body(field_ref, act_ref):
    normed, _ = normalize([field_ref[frame].astype(F32) for frame in range(2)])
    for frame in range(2):
        act_ref[frame] = (normed[frame] / (1.0 + jnp.exp(-normed[frame]))).astype(BF16)


def up_body(cot_ref, weight_ref, ahead_ref, local_ref, prior_ref):
    channels = cot_ref.shape[-1]
    weight = weight_ref[...]
    parts = []
    for frame in range(2):
        pair = jnp.concatenate([cot_ref[2 * frame], cot_ref[2 * frame + 1]], axis=1)
        parts.append(lax.dot_general(pair, weight, ROW_ROW, preferred_element_type=F32))
    first, second = parts
    low, mid, high = (slice(k * channels, (k + 1) * channels) for k in range(3))
    local_ref[0] = first[:, high] + second[:, mid]
    local_ref[1] = second[:, high]
    prior_ref[0] = first[:, low].astype(BF16)
    prior_ref[1] = (first[:, mid] + second[:, low]).astype(BF16)


def turn_body(weight_ref, out_ref):
    step = pl.program_id(0)
    for tap in range(3):
        at = step * 3 + tap
        out_ref[at] = weight_ref[26 - at].astype(F32).T.astype(BF16)


def fill_shifts(frames, cols_ref, breadth):
    rows, channels = frames[0].shape
    wide = lax.broadcasted_iota(jnp.int32, (rows, 1), 0) % breadth
    for at, frame in enumerate(frames):
        value = frame.astype(F32)
        for wide_tap in range(3):
            moved = value
            if wide_tap != 1:
                moved = pltpu.roll(value, (1 - wide_tap) % rows, 0)
                edge = 0 if wide_tap == 0 else breadth - 1
                moved = moved * jnp.where(wide == edge, 0.0, 1.0).astype(F32)
            for high_tap in range(3):
                shifted = moved
                if high_tap == 0:
                    shifted = jnp.concatenate(
                        [jnp.zeros((breadth, channels), F32), moved[: rows - breadth]], axis=0
                    )
                elif high_tap == 2:
                    shifted = jnp.concatenate(
                        [moved[breadth:], jnp.zeros((breadth, channels), F32)], axis=0
                    )
                tap = high_tap * 3 + wide_tap
                cols_ref[at * rows : (at + 1) * rows, tap * channels : (tap + 1) * channels] = (
                    shifted.astype(BF16)
                )


def accumulate(step, weight_ref, cols_ref, acc_ref):
    rows = acc_ref.shape[0]
    part = jnp.dot(
        cols_ref[pl.ds(pl.multiple_of(step * (rows // 2), rows // 2), rows), :],
        weight_ref[step],
        preferred_element_type=F32,
    )

    @pl.when(step == 0)
    def _():
        acc_ref[...] = part

    @pl.when(step > 0)
    def _():
        acc_ref[...] += part


def make_conv(breadth):
    def body(early_ref, late_ref, weight_ref, field_ref, hidden_ref, cols_ref, acc_ref):
        step = pl.program_id(0)

        @pl.when(step == 0)
        def _():
            frames = [early_ref[0], early_ref[1], late_ref[0], late_ref[1]]
            fill_shifts(frames, cols_ref, breadth)

        accumulate(step, weight_ref, cols_ref, acc_ref)

        @pl.when(step == 2)
        def _():
            rows = acc_ref.shape[0] // 2
            for frame in range(2):
                total = field_ref[frame].astype(F32) + acc_ref[frame * rows : (frame + 1) * rows]
                hidden_ref[frame] = total.astype(BF16)

    return body


def make_back(breadth):
    def body(
        early_ref, late_ref, weight_ref, field_ref, local_ref, next_ref, out_ref, cols_ref, acc_ref
    ):
        step = pl.program_id(0)

        @pl.when(step == 0)
        def _():
            frames = [early_ref[0], early_ref[1], late_ref[0], late_ref[1]]
            fill_shifts(frames, cols_ref, breadth)

        accumulate(step, weight_ref, cols_ref, acc_ref)

        @pl.when(step == 2)
        def _():
            rows = acc_ref.shape[0] // 2
            normed, scales = normalize([field_ref[frame].astype(F32) for frame in range(2)])
            grads = []
            for frame in range(2):
                gate = 1.0 / (1.0 + jnp.exp(-normed[frame]))
                slope = gate * (1.0 + normed[frame] * (1.0 - gate))
                grads.append(acc_ref[frame * rows : (frame + 1) * rows] * slope)
            means = group_means(grads + [grads[frame] * normed[frame] for frame in range(2)])
            for frame in range(2):
                inner = grads[frame] - means[frame] - normed[frame] * means[2 + frame]
                hidden_grad = local_ref[frame] + next_ref[frame].astype(F32)
                out_ref[frame] = (hidden_grad + scales[frame] * inner).astype(BF16)

    return body


def split_store(part, side, send_ref, keep_ref, times, at):
    rows, width = part.shape
    halves = part.reshape(times, rows // times, width)
    low = halves[:, : rows // times // 2]
    high = halves[:, rows // times // 2 :]
    send_ref[:, :, at : at + width] = jnp.where(side == 0, high, low).astype(BF16)
    keep_ref[:, :, at : at + width] = jnp.where(side == 0, low, high).astype(BF16)


def make_weight_grad(breadth, times):
    def body(early_ref, late_ref, grad_ref, send_ref, keep_ref, cols_ref, turned_ref):
        step = pl.program_id(0)
        rows, channels = early_ref.shape[1:]

        @pl.when(step == 0)
        def _():
            frames = [early_ref[0], early_ref[1], late_ref[0], late_ref[1]]
            fill_shifts(frames, cols_ref, breadth)
            for frame in range(2):
                turned_ref[:, frame * rows : (frame + 1) * rows] = (
                    grad_ref[frame].astype(F32).T.astype(BF16)
                )

        start = pl.multiple_of(step * rows, rows)
        turned = turned_ref[...]
        total = cols_ref.shape[1]
        for at in range(0, total, 2 * channels):
            width = min(2 * channels, total - at)
            part = jnp.dot(
                turned,
                cols_ref[pl.ds(start, 2 * rows), at : at + width],
                preferred_element_type=F32,
            )
            split_store(part, own_place()[3], send_ref, keep_ref, times, at)

    return body


def make_up_grad(times):
    def body(early_ref, late_ref, cot_ref, send_ref, keep_ref, cols_ref, turned_ref):
        rows, channels = early_ref.shape[1:]
        frames = [early_ref[0], early_ref[1], late_ref[0], late_ref[1]]
        for tap in range(3):
            for frame in range(2):
                cols_ref[
                    frame * rows : (frame + 1) * rows, tap * channels : (tap + 1) * channels
                ] = frames[frame + tap]
        for frame in range(2):
            for half in range(2):
                turned_ref[
                    half * channels : (half + 1) * channels, frame * rows : (frame + 1) * rows
                ] = cot_ref[2 * frame + half].astype(F32).T.astype(BF16)
        part = jnp.dot(turned_ref[...], cols_ref[...], preferred_element_type=F32)
        split_store(part, own_place()[3], send_ref, keep_ref, times, 0)

    return body


def swap_sides(value):
    return lax.ppermute(value, "dp", [(d, d ^ 1) for d in range(lax.axis_size("dp"))])


def place_of(device):
    time, data = divmod(device, 16)
    return [data // 4, time // 2, (data // 2 % 2) * 2 + time % 2, data % 2]


def device_at(x, y, z, core):
    return (y * 2 + z % 2) * 16 + x * 4 + z // 2 * 2 + core


def hop(piece, rings, step):
    pairs = []
    for device in range(128):
        place = place_of(device)
        ring = rings[place[3]]
        place[ring] = (place[ring] + step) % 4
        pairs.append((device, device_at(*place)))
    return lax.ppermute(piece, ("tm", "dp"), pairs)


def exchange(pieces, rings):
    return [pieces[0]] + [hop(pieces[at], rings, at) for at in (1, 2, 3)]


def added(refs):
    total = refs[0][...].astype(F32)
    for ref in refs[1:]:
        total = total + ref[...].astype(F32)
    return total


def pick(value, widths, index, count):
    parts, start = [], 0
    for width in widths:
        part = width // count
        parts.append(value[:, start + index * part : start + (index + 1) * part])
        start += width
    return jnp.concatenate(parts, axis=1)


def make_join(conv_rows, up_rows):
    widths = (conv_rows, up_rows, up_rows)

    def body(conv_got, conv_keep, up_got, up_keep, *refs):
        own_ref, ahead_ref, behind_ref, far_low_ref, far_high_ref, hold_ref = refs
        step = pl.program_id(0)
        x, y, _, core = own_place()
        conv = conv_got[0] + conv_keep[0]
        up = up_got[0] + up_keep[0]
        cols = conv.shape[1]
        for low in range(2):
            full = jnp.concatenate([conv[low], up[low, :cols], up[low, cols:]], axis=1)
            for at in range(4):
                hold_ref[at, low] = pick(full, widths, at, 4)
        near = ((0, own_ref), (1, ahead_ref), (3, behind_ref))
        far = lax.rem(x + 2, 4)

        @pl.when(core == 0)
        def _():
            for slot, ref in near:
                ref[step] = hold_ref[lax.rem(x + slot, 4)]

            @pl.when(step < 2)
            def _():
                far_low_ref[step] = hold_ref[far]

            @pl.when(step >= 2)
            def _():
                far_high_ref[step - 2] = hold_ref[far]

        turn = lax.rem(step - y + 4, 4)
        for slot, ref in near:

            @pl.when(jnp.logical_and(core == 1, turn == slot))
            def _():
                ref[...] = hold_ref[...]

        @pl.when(jnp.logical_and(core == 1, turn == 2))
        def _():
            far_low_ref[...] = hold_ref[0:2]
            far_high_ref[...] = hold_ref[2:4]

    return body


def make_relay(conv_rows, up_rows):
    def body(ahead_ref, behind_ref, low_ref, high_ref, ahead_out, behind_out):
        ahead_out[0:2] = ahead_ref[0:2] + low_ref[...]
        ahead_out[2:4] = ahead_ref[2:4]
        behind_out[0:2] = behind_ref[0:2]
        behind_out[2:4] = behind_ref[2:4] + high_ref[...]

    return body


def make_mid(conv_rows, up_rows):
    def body(*refs):
        outs, hold_ref = refs[3:7], refs[7]
        x, y, _, core = own_place()
        hold_ref[...] = added(refs[:3])
        other = jnp.where(core == 0, y, x)
        for slot in range(4):
            outs[slot][...] = hold_ref[lax.rem(other + slot, 4)].astype(outs[slot].dtype)

    return body


def make_end(conv_rows, up_rows):
    widths = (conv_rows // 4, up_rows // 4, up_rows // 4)

    def body(*refs):
        outs, hold_ref = refs[4:8], refs[8]
        total = added(refs[:4])
        for low in range(2):
            for high in range(2):
                hold_ref[high * 2 + low] = pick(total[low], widths, high, 2)
        for slot in range(4):
            outs[slot][...] = hold_ref[lax.rem(own_place()[2] + slot, 4)].astype(outs[slot].dtype)

    return body


def make_last(conv_rows, up_rows):
    widths = (conv_rows // 8, up_rows // 8, up_rows // 8)

    def body(*refs):
        total = added(refs[:4])
        low, high = pick(total, widths, 0, 2), pick(total, widths, 1, 2)
        refs[4][...] = jnp.where(own_place()[3] == 0, low, high)
        refs[5][...] = jnp.where(own_place()[3] == 0, high, low)

    return body


def make_spread(conv_rows, up_rows, scale):
    cut, part = conv_rows // 16, up_rows // 16

    def body(mine_ref, got_ref, conv_ref, up_ref):
        even = own_place()[3] == 0
        mine, got = mine_ref[...], got_ref[...]
        sides = jnp.where(even, mine, got), jnp.where(even, got, mine)
        conv_ref[...] = jnp.concatenate([side[:, :cut] for side in sides], axis=0) * scale
        pieces = [
            side[:, cut + at * part : cut + (at + 1) * part] for side in sides for at in range(2)
        ]
        up_ref[...] = jnp.concatenate(pieces, axis=0).T * scale

    return body


def reduce_blocks(conv_send, conv_keep, up_send, up_keep, scale):
    times, cols, conv_rows = conv_send.shape
    up_rows = up_send.shape[2]
    rows = conv_rows + 2 * up_rows

    def small(make, arrays, shapes, scratch):
        return call(
            make(conv_rows, up_rows),
            (1,),
            [RESIDENT] * len(arrays),
            [RESIDENT] * len(shapes),
            shapes,
            scratch,
            flops=1000,
            nbytes=2 * times * cols * rows,
        )(*arrays)

    def shape(*dims):
        return jax.ShapeDtypeStruct(dims, BF16)

    def slots(*dims):
        return [jax.ShapeDtypeStruct(dims, F32)] + [jax.ShapeDtypeStruct(dims, BF16)] * 3

    conv_got = swap_sides(conv_send)
    up_got = swap_sides(up_send)
    conv_blocks = (4, 2, cols, conv_rows)
    up_blocks = (4, 2, 2 * cols, up_rows)
    conv_spec = pl.BlockSpec((1,) + conv_blocks[1:], lambda k: (k, 0, 0, 0))
    up_spec = pl.BlockSpec((1,) + up_blocks[1:], lambda k: (k, 0, 0, 0))
    quarter = (2, cols, rows // 4)
    out = call(
        make_join(conv_rows, up_rows),
        (4,),
        [conv_spec, conv_spec, up_spec, up_spec],
        [whole(4, *quarter)] * 3 + [whole(2, *quarter)] * 2,
        [shape(4, *quarter)] * 3 + [shape(2, *quarter)] * 2,
        [pltpu.VMEM((4,) + quarter, BF16)],
        flops=1000,
        nbytes=6 * times * cols * rows,
    )(
        conv_got.reshape(conv_blocks),
        conv_keep.reshape(conv_blocks),
        up_got.reshape(up_blocks),
        up_keep.reshape(up_blocks),
    )
    own, ahead, behind, far_low, far_high = out
    far_low = hop(far_low, (0, 1), 1)
    far_high = hop(far_high, (0, 1), 3)
    ahead, behind = small(
        make_relay, [ahead, behind, far_low, far_high], [shape(4, *quarter)] * 2, []
    )
    ahead = hop(ahead, (0, 1), 1)
    behind = hop(behind, (0, 1), 3)
    out = small(make_mid, [own, ahead, behind], slots(*quarter), [pltpu.VMEM((4,) + quarter, F32)])
    out = exchange(out, (1, 0))
    hold = pltpu.VMEM((4, cols, rows // 8), F32)
    out = small(make_end, out, slots(cols, rows // 8), [hold])
    out = exchange(out, (2, 2))
    half = jax.ShapeDtypeStruct((cols, rows // 16), F32)
    mine, other = small(make_last, out, [half, half], [])
    got = swap_sides(other)
    cut, part = conv_rows // 16, up_rows // 16
    return small(
        lambda *sizes: make_spread(*sizes, scale),
        [mine, got],
        [
            jax.ShapeDtypeStruct((2 * cols, cut), F32),
            jax.ShapeDtypeStruct((part, 4 * cols), F32),
        ],
        [],
    )


def step(features, conv_weight, up_weight, cotangent):
    crops, frames, height, breadth, channels = features.shape
    rows = height * breadth
    times = lax.axis_size("tm")
    data = lax.axis_size("dp")
    scale = 1.0 / math.sqrt(crops * frames * rows * times * data)
    field = features.reshape(frames, rows, channels)
    cot = cotangent.reshape(2 * frames, rows, channels)
    block = (frames, rows, channels)
    square = 2 * channels * channels
    act = call(
        act_body,
        (1,),
        [whole(*block)],
        whole(*block),
        jax.ShapeDtypeStruct(block, BF16),
        flops=20 * frames * rows * channels,
        nbytes=4 * frames * rows * channels,
    )(field)
    act_prior = from_behind(act, "tm", 1)
    local, prior_part = call(
        up_body,
        (1,),
        [whole(*cot.shape), whole(*up_weight.shape), RESIDENT],
        [whole(*block), whole(*block)],
        [jax.ShapeDtypeStruct(block, F32), jax.ShapeDtypeStruct(block, BF16)],
        flops=6 * frames * rows * square,
        nbytes=10 * frames * rows * channels,
    )(cot, up_weight, conv_weight)
    next_part = from_behind(prior_part, "tm", -1)
    taps = conv_weight.reshape(27, channels, channels)
    turned = call(
        turn_body,
        (9,),
        [RESIDENT],
        RESIDENT,
        jax.ShapeDtypeStruct(taps.shape, BF16),
        flops=27 * square,
        nbytes=4 * 27 * channels * channels,
    )(taps)
    turned = turned.reshape(3, 9 * channels, channels)
    conv_grad = (local + next_part.astype(F32)).astype(BF16)
    conv_next = from_behind(conv_grad, "tm", -1)
    columns = pltpu.VMEM((4 * rows, 9 * channels), BF16)
    sums = pltpu.VMEM((frames * rows, channels), F32)
    hidden = call(
        make_conv(breadth),
        (3,),
        [whole(*block), whole(*block), RESIDENT, whole(*block)],
        whole(*block),
        jax.ShapeDtypeStruct(block, BF16),
        [columns, sums],
        flops=27 * frames * rows * square,
        nbytes=2 * 27 * channels * channels,
    )(act_prior, act, conv_weight.reshape(3, 9 * channels, channels), field)
    hidden_prior = from_behind(hidden, "tm", 1)
    cut = channels // times // 2
    half = jax.ShapeDtypeStruct((times, cut, 27 * channels), BF16)
    half_spec = pl.BlockSpec((times, cut, 9 * channels), lambda k: (0, 0, k))
    send, keep = call(
        make_weight_grad(breadth, times),
        (3,),
        [whole(*block), whole(*block), whole(*block)],
        [half_spec, half_spec],
        [half, half],
        [columns, pltpu.VMEM((channels, frames * rows), BF16)],
        flops=27 * frames * rows * square,
        nbytes=4 * 27 * channels * channels,
    )(act_prior, act, conv_grad)
    up_half = jax.ShapeDtypeStruct((times, channels // times, 3 * channels), BF16)
    up_send, up_keep = call(
        make_up_grad(times),
        (1,),
        [whole(*block), whole(*block), whole(*cot.shape)],
        [whole(*up_half.shape), whole(*up_half.shape)],
        [up_half, up_half],
        [
            pltpu.VMEM((frames * rows, 3 * channels), BF16),
            pltpu.VMEM((2 * channels, frames * rows), BF16),
        ],
        flops=6 * frames * rows * square,
        nbytes=12 * channels * channels,
    )(hidden_prior, hidden, cot)
    grad_conv, grad_up = reduce_blocks(send, keep, up_send, up_keep, scale)
    features_grad = call(
        make_back(breadth),
        (3,),
        [whole(*block), whole(*block), RESIDENT] + [whole(*block)] * 3,
        whole(*block),
        jax.ShapeDtypeStruct(block, BF16),
        [columns, sums],
        flops=27 * frames * rows * square,
        nbytes=2 * 27 * channels * channels,
    )(conv_grad, conv_next, turned, field, local, next_part)
    return (features_grad.reshape(features.shape), grad_conv.T, grad_up)


def solution(mesh):
    in_specs = (P("dp", "tm", None, None, None), P(), P(), P("dp", "tm", None, None, None))
    out_specs = (P("dp", "tm", None, None, None), P("dp", "tm"), P("dp", "tm"))
    return jax.shard_map(step, mesh=mesh, in_specs=in_specs, out_specs=out_specs, check_vma=False)
```
